32 devices in a mesh: grp: 2 (over x), blk: 8 (over z, y), sub: 2 (over core).
Axes of the slice: x: 2, y: 2, z: 4, core: 2. Of those that a mesh axis runs over, the one named last changes fastest.
Arguments:
- spectra: bfloat16 [16, 2, 256, 2048], P('sub', None, None, ('grp', 'blk')), parts along dimension 3, may hold values from -6 to 6
- direction: int32 [2, 8], P(None, 'blk'), may hold values 0 or 1
Outputs:
- correlations: float32 [2, 16, 64, 128, 128], P(None, ('grp', 'blk'), 'sub'), parts along dimension 1
The draws below stay inside these ranges and needn't reach their ends.
There are 2 independent parts, one for each index of `grp`. The reference program is written for one: setup_inputs(seed, part) draws one part's arguments, and reference() takes and returns one part's arrays. A program takes and returns all parts, laid end to end along the dimension named above; an argument that names none is the same for every part. Nothing has to cross between parts.
Inputs may be any that keep to these rules, and one draw needn't show every extreme that they name: direction[r, b] = 1 puts block b's partner in round r at block b + r + 1, 0 at block b - r - 1, modulo 8.
All inputs are finite; a program needn't handle non-finite values.
Results may differ from the reference program's by a relative error of at most 0.011.
Values may be sent and summed in bfloat16 or wider, within the bound.
A program may use at most 128 MiB of HBM per device.

```python
import math
import jax
import jax.numpy as jnp
from jax import lax

CB = 128
F = 256
LAGS = 64
ROUNDS = 2
NB = 8
C = 1024
S = 16


def touch_ends(values, rng, smallest, top_value):
    place = [jax.random.randint(jax.random.fold_in(rng, axis), (), 0, length) for axis, length in enumerate(values.shape)]
    widest = values.shape.index(max(values.shape))
    next_to = place[:widest] + [(place[widest] + 1) % values.shape[widest]] + place[widest + 1:]
    return values.at[tuple(place)].set(smallest).at[tuple(next_to)].set(top_value)


def level_of(key, dims, split, smallest, top_value):
    factor_of, own = 1.0, jax.random.fold_in(key, 6)
    for axis_at, shards_of in split:
        draws = jnp.exp(jax.random.uniform(jax.random.fold_in(own, axis_at), (shards_of,), jnp.float32, smallest / len(split), top_value / len(split)))
        factor_of = factor_of * jnp.repeat(draws, dims[axis_at] // shards_of).reshape([-1 if axis == axis_at else 1 for axis in range(len(dims))])
    return factor_of


def bell_draw(stream_key, extent, scale, bound, split=(), held_as=jnp.bfloat16):
    drawn = jax.random.normal(stream_key, extent, jnp.float32) * scale
    if len(split) > 0:
        drawn = level_of(stream_key, extent, split, -0.22, 0.18) * drawn
    return jnp.clip(drawn, min=-bound, max=bound).astype(held_as)


def setup_inputs(seed: int = 0, part: int = 0) -> dict:
    arg_keys = jax.random.split(jax.random.key(seed), 3)
    part_keys = jax.random.split(jax.random.fold_in(arg_keys[2], part), 3)
    return {
        "spectra": bell_draw(part_keys[0], (S, 2, F, C), 1.0, 6.0, ((0, 2), (3, 8))),
        "direction": touch_ends((jax.random.randint(arg_keys[1], (ROUNDS, NB), 0, 2) < 1).astype(jnp.int32), jax.random.fold_in(arg_keys[1], 1), 0, 1),
    }


def make_table(bin_count, windows, lag_count):
    lags = jnp.arange(lag_count, dtype=jnp.int32) - lag_count // 2
    bins = jnp.arange(bin_count, dtype=jnp.int32)
    period = 2 * bin_count
    phase = (bins[None, :] * ((lags[:, None] + period) % period)) % period
    angle = phase.astype(jnp.float32) * (math.pi / bin_count)
    weight = (bin_count * windows) ** -0.5
    return (jnp.stack([jnp.cos(angle), -jnp.sin(angle)], axis=-1) * weight).astype(jnp.bfloat16)


def reference(spectra, direction):
    blocks = spectra.reshape(S, 2, F, NB, CB)
    lag_table = make_table(F, S, LAGS).astype(jnp.float32)
    rounds_out = []
    for round_index in range(ROUNDS):
        def one_block(block_index):
            sign = 2 * direction[round_index, block_index] - 1
            partner_index = ((block_index + NB + sign * (round_index + 1)) % NB).astype(jnp.int32)
            local_block = lax.dynamic_index_in_dim(blocks, block_index.astype(jnp.int32), 3, keepdims=False)
            partner = lax.dynamic_index_in_dim(blocks, partner_index, 3, keepdims=False)
            swapped = jnp.stack([partner[:, 1], -partner[:, 0]], axis=1)
            operand = jnp.concatenate([partner, swapped], axis=-1)
            cross_tile = jnp.einsum("scfi,scfj->fij", local_block.astype(jnp.float32), operand.astype(jnp.float32))
            cross_tile = cross_tile.astype(jnp.bfloat16).astype(jnp.float32).reshape(F, CB, 2, CB)
            return jnp.einsum("tfk,fikj->tij", lag_table, cross_tile)
        rounds_out.append(lax.map(one_block, jnp.arange(NB, dtype=jnp.int32)))
    return jnp.stack(rounds_out, axis=0)
```

```python
import math

import jax
import jax.numpy as jnp
from jax import lax
from jax.sharding import PartitionSpec as P

LAGS = 64
ROUNDS = 2


def from_behind(x, axis, by):
    size = lax.axis_size(axis)
    return lax.ppermute(x, axis, [(i, (i + by) % size) for i in range(size)])


def make_table(bin_count, windows, lag_count):
    lags = jnp.arange(lag_count, dtype=jnp.int32) - lag_count // 2
    bins = jnp.arange(bin_count, dtype=jnp.int32)
    period = 2 * bin_count
    phase = bins[None, :] * ((lags[:, None] + period) % period) % period
    angle = phase.astype(jnp.float32) * (math.pi / bin_count)
    weight = (bin_count * windows) ** (-0.5)
    return (jnp.stack([jnp.cos(angle), -jnp.sin(angle)], axis=-1) * weight).astype(jnp.bfloat16)


def correlate(left, partner, flat_table):
    bin_count, channels = partner.shape[2], partner.shape[3]
    cross = jnp.einsum("dscfi,scfk->fdik", left, partner, preferred_element_type=jnp.float32)
    cross = cross.astype(jnp.bfloat16).reshape(bin_count * 2, channels, channels)
    return jnp.einsum("tx,xik->tik", flat_table, cross, preferred_element_type=jnp.float32)


def per_device(spectra, direction):
    windows, _, bin_count, channels = spectra.shape
    lag_table = make_table(bin_count, windows * lax.axis_size("sub"), LAGS)
    flat_table = lag_table.reshape(LAGS, bin_count * 2)
    real, imag = spectra[:, 0], spectra[:, 1]
    left = jnp.stack(
        [jnp.stack([real, imag], axis=1), jnp.stack([-imag, real], axis=1)], axis=0
    )
    reduced_rounds = []
    for round_index in range(ROUNDS):
        ahead = from_behind(spectra, "blk", -(round_index + 1))
        behind = from_behind(spectra, "blk", round_index + 1)
        partner = jnp.where(direction[round_index, 0] == 1, ahead, behind)
        partial_lags = correlate(left, partner, flat_table)
        reduced_rounds.append(
            lax.psum_scatter(
                partial_lags.astype(jnp.bfloat16), "sub", scatter_dimension=0, tiled=True
            ).astype(jnp.float32)
        )
    reduced = jnp.stack(reduced_rounds, axis=0)
    return reduced[:, None]


def solution(mesh):
    return jax.shard_map(
        per_device,
        mesh=mesh,
        in_specs=(P("sub", None, None, ("grp", "blk")), P(None, "blk")),
        out_specs=P(None, ("grp", "blk"), "sub", None, None),
        check_vma=False,
    )
```

```python
import math

import jax
import jax.numpy as jnp
from jax import lax
from jax.sharding import PartitionSpec as P

LAGS = 64
ROUNDS = 2


def from_behind(x, axis, by):
    size = lax.axis_size(axis)
    return lax.ppermute(x, axis, [(i, (i + by) % size) for i in range(size)])


def make_table(bin_count, windows, lag_count):
    lags = jnp.arange(lag_count, dtype=jnp.int32) - lag_count // 2
    bins = jnp.arange(bin_count, dtype=jnp.int32)
    period = 2 * bin_count
    phase = bins[None, :] * ((lags[:, None] + period) % period) % period
    angle = phase.astype(jnp.float32) * (math.pi / bin_count)
    weight = (bin_count * windows) ** (-0.5)
    return (jnp.stack([jnp.cos(angle), -jnp.sin(angle)], axis=-1) * weight).astype(jnp.bfloat16)


def correlate(left, partner, flat_table):
    bin_count, channels = partner.shape[2], partner.shape[3]
    cross = jnp.einsum("dscfi,scfk->fdik", left, partner, preferred_element_type=jnp.float32)
    cross = cross.astype(jnp.bfloat16).reshape(bin_count * 2, channels, channels)
    return jnp.einsum("tx,xik->tik", flat_table, cross, preferred_element_type=jnp.float32)


def per_device(spectra, direction):
    windows, _, bin_count, channels = spectra.shape
    lag_table = make_table(bin_count, windows * lax.axis_size("sub"), LAGS)
    flat_table = lag_table.reshape(LAGS, bin_count * 2)
    real, imag = spectra[:, 0], spectra[:, 1]
    left = jnp.stack(
        [jnp.stack([real, imag], axis=1), jnp.stack([-imag, real], axis=1)], axis=0
    )
    received = []
    for round_index in range(ROUNDS):
        received.append(from_behind(spectra, "blk", -(round_index + 1)))
        received.append(from_behind(spectra, "blk", round_index + 1))
    received = lax.optimization_barrier(tuple(received))
    reduced_rounds = []
    for round_index in range(ROUNDS):
        ahead, behind = received[2 * round_index], received[2 * round_index + 1]
        partner = jnp.where(direction[round_index, 0] == 1, ahead, behind)
        partial_lags = correlate(left, partner, flat_table)
        reduced_rounds.append(
            lax.psum_scatter(
                partial_lags.astype(jnp.bfloat16), "sub", scatter_dimension=0, tiled=True
            ).astype(jnp.float32)
        )
    reduced = jnp.stack(reduced_rounds, axis=0)
    return reduced[:, None]


def solution(mesh):
    return jax.shard_map(
        per_device,
        mesh=mesh,
        in_specs=(P("sub", None, None, ("grp", "blk")), P(None, "blk")),
        out_specs=P(None, ("grp", "blk"), "sub", None, None),
        check_vma=False,
    )
```

```python
import math

import jax
import jax.numpy as jnp
from jax import lax
from jax.sharding import PartitionSpec as P

LAGS = 64
ROUNDS = 2


def from_behind(x, axis, by):
    size = lax.axis_size(axis)
    return lax.ppermute(x, axis, [(i, (i + by) % size) for i in range(size)])


def make_table(bin_count, windows, lag_count):
    lags = jnp.arange(lag_count, dtype=jnp.int32) - lag_count // 2
    bins = jnp.arange(bin_count, dtype=jnp.int32)
    period = 2 * bin_count
    phase = bins[None, :] * ((lags[:, None] + period) % period) % period
    angle = phase.astype(jnp.float32) * (math.pi / bin_count)
    weight = (bin_count * windows) ** (-0.5)
    return (jnp.stack([jnp.cos(angle), -jnp.sin(angle)], axis=-1) * weight).astype(jnp.bfloat16)


def correlate(left, partner, flat_table):
    bin_count, channels = partner.shape[2], partner.shape[3]
    cross = jnp.einsum("dscfi,scfk->fdik", left, partner, preferred_element_type=jnp.float32)
    cross = cross.astype(jnp.bfloat16).reshape(bin_count * 2, channels, channels)
    return jnp.einsum("tx,xik->tik", flat_table, cross, preferred_element_type=jnp.float32)


def per_device(spectra, direction):
    windows, _, bin_count, channels = spectra.shape
    lag_table = make_table(bin_count, windows * lax.axis_size("sub"), LAGS)
    half = bin_count // 2
    halves = (spectra[:, :, :half], spectra[:, :, half:])
    received = []
    for chunk_index, chunk in enumerate(halves):
        if chunk_index > 0:
            chunk = lax.optimization_barrier((received[-1], chunk))[1]
        moved = []
        for round_index in range(ROUNDS):
            moved.append(from_behind(chunk, "blk", -(round_index + 1)))
            moved.append(from_behind(chunk, "blk", round_index + 1))
        received.append(lax.optimization_barrier(tuple(moved)))
    summed = [None] * ROUNDS
    for chunk_index, chunk in enumerate(halves):
        flat_table = lag_table[:, chunk_index * half : (chunk_index + 1) * half].reshape(LAGS, half * 2)
        real, imag = chunk[:, 0], chunk[:, 1]
        left = jnp.stack(
            [jnp.stack([real, imag], axis=1), jnp.stack([-imag, real], axis=1)], axis=0
        )
        for round_index in range(ROUNDS):
            ahead = received[chunk_index][2 * round_index]
            behind = received[chunk_index][2 * round_index + 1]
            partner = jnp.where(direction[round_index, 0] == 1, ahead, behind)
            part = correlate(left, partner, flat_table)
            summed[round_index] = part if summed[round_index] is None else summed[round_index] + part
    reduced_rounds = [
        lax.psum_scatter(
            partial_lags.astype(jnp.bfloat16), "sub", scatter_dimension=0, tiled=True
        ).astype(jnp.float32)
        for partial_lags in summed
    ]
    reduced = jnp.stack(reduced_rounds, axis=0)
    return reduced[:, None]


def solution(mesh):
    return jax.shard_map(
        per_device,
        mesh=mesh,
        in_specs=(P("sub", None, None, ("grp", "blk")), P(None, "blk")),
        out_specs=P(None, ("grp", "blk"), "sub", None, None),
        check_vma=False,
    )
```

```python
import math

import jax
import jax.numpy as jnp
from jax import lax
from jax.sharding import PartitionSpec as P

LAGS = 64
ROUNDS = 2
CHUNKS = 4


def from_behind(x, axis, by):
    size = lax.axis_size(axis)
    return lax.ppermute(x, axis, [(i, (i + by) % size) for i in range(size)])


def make_table(bin_count, windows, lag_count):
    lags = jnp.arange(lag_count, dtype=jnp.int32) - lag_count // 2
    bins = jnp.arange(bin_count, dtype=jnp.int32)
    period = 2 * bin_count
    phase = bins[None, :] * ((lags[:, None] + period) % period) % period
    angle = phase.astype(jnp.float32) * (math.pi / bin_count)
    weight = (bin_count * windows) ** (-0.5)
    return (jnp.stack([jnp.cos(angle), -jnp.sin(angle)], axis=-1) * weight).astype(jnp.bfloat16)


def correlate(left, partner, flat_table):
    bin_count, channels = partner.shape[2], partner.shape[3]
    cross = jnp.einsum("dscfi,scfk->fdik", left, partner, preferred_element_type=jnp.float32)
    cross = cross.astype(jnp.bfloat16).reshape(bin_count * 2, channels, channels)
    return jnp.einsum("tx,xik->tik", flat_table, cross, preferred_element_type=jnp.float32)


def per_device(spectra, direction):
    windows, _, bin_count, channels = spectra.shape
    lag_table = make_table(bin_count, windows * lax.axis_size("sub"), LAGS)
    half = bin_count // CHUNKS
    halves = [spectra[:, :, c * half : (c + 1) * half] for c in range(CHUNKS)]
    received = []
    for chunk_index, chunk in enumerate(halves):
        if chunk_index > 0:
            chunk = lax.optimization_barrier((received[-1], chunk))[1]
        moved = []
        for round_index in range(ROUNDS):
            moved.append(from_behind(chunk, "blk", -(round_index + 1)))
            moved.append(from_behind(chunk, "blk", round_index + 1))
        received.append(lax.optimization_barrier(tuple(moved)))
    summed = [None] * ROUNDS
    for chunk_index, chunk in enumerate(halves):
        flat_table = lag_table[:, chunk_index * half : (chunk_index + 1) * half].reshape(LAGS, half * 2)
        real, imag = chunk[:, 0], chunk[:, 1]
        left = jnp.stack(
            [jnp.stack([real, imag], axis=1), jnp.stack([-imag, real], axis=1)], axis=0
        )
        for round_index in range(ROUNDS):
            ahead = received[chunk_index][2 * round_index]
            behind = received[chunk_index][2 * round_index + 1]
            partner = jnp.where(direction[round_index, 0] == 1, ahead, behind)
            part = correlate(left, partner, flat_table)
            summed[round_index] = part if summed[round_index] is None else summed[round_index] + part
    reduced_rounds = [
        lax.psum_scatter(
            partial_lags.astype(jnp.bfloat16), "sub", scatter_dimension=0, tiled=True
        ).astype(jnp.float32)
        for partial_lags in summed
    ]
    reduced = jnp.stack(reduced_rounds, axis=0)
    return reduced[:, None]


def solution(mesh):
    return jax.shard_map(
        per_device,
        mesh=mesh,
        in_specs=(P("sub", None, None, ("grp", "blk")), P(None, "blk")),
        out_specs=P(None, ("grp", "blk"), "sub", None, None),
        check_vma=False,
    )
```

```python
import math

import jax
import jax.numpy as jnp
from jax import lax
from jax.sharding import PartitionSpec as P

LAGS = 64
ROUNDS = 2


def from_behind(x, axis, by):
    size = lax.axis_size(axis)
    return lax.ppermute(x, axis, [(i, (i + by) % size) for i in range(size)])


def make_table(bin_count, windows, lag_count):
    lags = jnp.arange(lag_count, dtype=jnp.int32) - lag_count // 2
    bins = jnp.arange(bin_count, dtype=jnp.int32)
    period = 2 * bin_count
    phase = bins[None, :] * ((lags[:, None] + period) % period) % period
    angle = phase.astype(jnp.float32) * (math.pi / bin_count)
    weight = (bin_count * windows) ** (-0.5)
    return (jnp.stack([jnp.cos(angle), -jnp.sin(angle)], axis=-1) * weight).astype(jnp.bfloat16)


def correlate(left, partner, flat_table):
    bin_count, channels = partner.shape[2], partner.shape[3]
    cross = jnp.einsum("dscfi,scfk->fdik", left, partner, preferred_element_type=jnp.float32)
    cross = cross.astype(jnp.bfloat16).reshape(bin_count * 2, channels, channels)
    return jnp.einsum("tx,xik->tik", flat_table, cross, preferred_element_type=jnp.float32)


def per_device(spectra, direction):
    windows, _, bin_count, channels = spectra.shape
    lag_table = make_table(bin_count, windows * lax.axis_size("sub"), LAGS)
    cuts = (0, bin_count // 4, bin_count)
    halves = [spectra[:, :, cuts[c] : cuts[c + 1]] for c in range(2)]
    received = []
    for chunk_index, chunk in enumerate(halves):
        if chunk_index > 0:
            chunk = lax.optimization_barrier((received[-1], chunk))[1]
        moved = []
        for round_index in range(ROUNDS):
            moved.append(from_behind(chunk, "blk", -(round_index + 1)))
            moved.append(from_behind(chunk, "blk", round_index + 1))
        received.append(lax.optimization_barrier(tuple(moved)))
    summed = [None] * ROUNDS
    for chunk_index, chunk in enumerate(halves):
        width = cuts[chunk_index + 1] - cuts[chunk_index]
        flat_table = lag_table[:, cuts[chunk_index] : cuts[chunk_index + 1]].reshape(LAGS, width * 2)
        real, imag = chunk[:, 0], chunk[:, 1]
        left = jnp.stack(
            [jnp.stack([real, imag], axis=1), jnp.stack([-imag, real], axis=1)], axis=0
        )
        for round_index in range(ROUNDS):
            ahead = received[chunk_index][2 * round_index]
            behind = received[chunk_index][2 * round_index + 1]
            partner = jnp.where(direction[round_index, 0] == 1, ahead, behind)
            part = correlate(left, partner, flat_table)
            summed[round_index] = part if summed[round_index] is None else summed[round_index] + part
    reduced_rounds = [
        lax.psum_scatter(
            partial_lags.astype(jnp.bfloat16), "sub", scatter_dimension=0, tiled=True
        ).astype(jnp.float32)
        for partial_lags in summed
    ]
    reduced = jnp.stack(reduced_rounds, axis=0)
    return reduced[:, None]


def solution(mesh):
    return jax.shard_map(
        per_device,
        mesh=mesh,
        in_specs=(P("sub", None, None, ("grp", "blk")), P(None, "blk")),
        out_specs=P(None, ("grp", "blk"), "sub", None, None),
        check_vma=False,
    )
```
